32 devices in a mesh: groups: 2 (over x), depth: 16 (over z, y, core).
Axes of the slice: x: 2, y: 2, z: 4, core: 2. Of those that a mesh axis runs over, the one named last changes fastest.
Arguments:
- object_slices: bfloat16 [32, 2, 512, 512], P(('groups', 'depth')), parts along dimension 0, may hold values from -1 to 1, as said below
- probes: float32 [8, 2, 128, 128], P('groups'), parts along dimension 0, may hold values from -4 to 4
- measured: float32 [16, 128, 128], P('groups'), parts along dimension 0, may hold values from 0.05 to 5
- scan_offsets: int32 [16, 2], P('groups'), parts along dimension 0, may hold values from 0 to 384
- probe_ids: int32 [16], P('groups'), parts along dimension 0, may hold values from 0 to 3
Outputs:
- object_grad: bfloat16 [32, 2, 512, 512], P(('groups', 'depth')), parts along dimension 0
The draws below stay inside these ranges and needn't reach their ends.
There are 2 independent parts, one for each index of `groups`. The reference program is written for one: setup_inputs(seed, part) draws one part's arguments, and reference() takes and returns one part's arrays. A program takes and returns all parts, laid end to end along the dimension named above; each array names one. Nothing has to cross between parts.
Inputs may be any that keep to these rules, and one draw needn't show every extreme that they name: `scan_offsets`: row and column of the first pixel of each position's window in the object. `probe_ids`: the probe state used at each position. `object_slices`: real and imaginary parts of a transmission whose modulus is at most 1.
All inputs are finite; a program needn't handle non-finite values.
Results may differ from the reference program's by a relative error of at most 0.001.
Values sent between devices are 32-bit elements; how exact they have to be, the bound alone decides.
A program may use at most 64 MiB of HBM per device.

```python
import math
import jax
import jax.numpy as jnp
from jax import lax

WIN = 128
OBJ = 512
POS = 8
NPROBE = 4
NSLICE = 16


def draw_object_slices(key, part):
    key_damping, key_phase = jax.random.split(jax.random.fold_in(key, 17))
    damping = jax.random.uniform(key_damping, (NSLICE, OBJ, OBJ), jnp.float32, 0.0, 0.01)
    phase_shift = jax.random.uniform(key_phase, (NSLICE, OBJ, OBJ), jnp.float32, -1.0, 1.0)
    modulus = jnp.exp(-damping)
    return jnp.stack([modulus * jnp.cos(phase_shift), modulus * jnp.sin(phase_shift)], 1).astype(jnp.bfloat16)


def touch_ends(result, stream_key, low, largest):
    longest = result.shape.index(max(result.shape))
    spots = []
    for shift in (0, 1):
        where = [jax.random.randint(jax.random.fold_in(stream_key, axis), (), 0, length) for axis, length in enumerate(result.shape)]
        where[longest] = (where[longest] + shift) % result.shape[longest]
        spots.append(tuple(where))
    return result.at[spots[0]].set(low).at[spots[1]].set(largest)


def gaussian(rng, shape, deviation, reach, held_as=jnp.bfloat16):
    result = jax.random.normal(rng, shape, jnp.float32) * deviation
    return jnp.minimum(jnp.maximum(result, -reach), reach).astype(held_as)


def setup_inputs(seed: int = 0, part: int = 0) -> dict:
    splits = jax.random.split(jax.random.key(seed), 6)
    part_keys = jax.random.split(jax.random.fold_in(splits[5], part), 6)
    return {
        "object_slices": draw_object_slices(jax.random.fold_in(jax.random.fold_in(splits[5], part), 71), part),
        "probes": gaussian(part_keys[1], (NPROBE, 2, WIN, WIN), 0.7, 4.0, jnp.float32),
        "measured": jnp.clip(jnp.exp(jax.random.uniform(part_keys[2], (POS, WIN, WIN), jnp.float32, math.log(0.05), math.log(5.0))), 0.05, 5.0),
        "scan_offsets": touch_ends(jax.random.randint(part_keys[3], (POS, 2), 0, OBJ - WIN + 1), jax.random.fold_in(part_keys[3], 1), 0, OBJ - WIN).astype(jnp.int32),
        "probe_ids": touch_ends(jax.random.randint(part_keys[4], (POS,), 0, NPROBE), jax.random.fold_in(part_keys[4], 1), 0, NPROBE - 1).astype(jnp.int32),
    }


def dft_tables(length):
    ordinal = jnp.arange(length, dtype=jnp.int32)
    products = ordinal[:, None] * ordinal[None, :] % length
    phase_angle = products.astype(jnp.float32) * (2.0 * math.pi / length)
    factor = 1.0 / math.sqrt(length)
    return (jnp.cos(phase_angle) * factor, -jnp.sin(phase_angle) * factor)

def kernel_table(length):
    ordinal = jnp.arange(length, dtype=jnp.int32)
    spatial = jnp.where(ordinal < length // 2, ordinal, ordinal - length)
    squares = (spatial[:, None] * spatial[:, None] + spatial[None, :] * spatial[None, :]) % (2 * length)
    phase_angle = squares.astype(jnp.float32) * (math.pi / length)
    return (jnp.cos(phase_angle), -jnp.sin(phase_angle))

def matmul_last(values, table):
    return jnp.einsum('bxk,kc->bxc', values, table, precision=lax.Precision.HIGHEST)

def matmul_first(table, values):
    return jnp.einsum('rj,bjc->brc', table, values, precision=lax.Precision.HIGHEST)

def transform(field_in, table_real, table_imag):
    real_part = field_in[:, 0]
    imag_part = field_in[:, 1]
    mid_real = matmul_last(real_part, table_real) - matmul_last(imag_part, table_imag)
    mid_imag = matmul_last(real_part, table_imag) + matmul_last(imag_part, table_real)
    out_real = matmul_first(table_real, mid_real) - matmul_first(table_imag, mid_imag)
    out_imag = matmul_first(table_real, mid_imag) + matmul_first(table_imag, mid_real)
    return (out_real, out_imag)

def complex_mul(left_real, left_imag, right_real, right_imag):
    return (left_real * right_real - left_imag * right_imag, left_real * right_imag + left_imag * right_real)

def cut_windows(object_slab, offsets):
    zero_index = jnp.zeros((), jnp.int32)

    def one_window(corner):
        return lax.dynamic_slice(object_slab, (zero_index, corner[0].astype(jnp.int32), corner[1].astype(jnp.int32)), (2, WIN, WIN))
    return jax.vmap(one_window)(offsets)

def paint(grad_field, offsets):
    zero_index = jnp.zeros((), jnp.int32)

    def add_one(position, image):
        corner_at = (zero_index, offsets[position, 0].astype(jnp.int32), offsets[position, 1].astype(jnp.int32))
        current = lax.dynamic_slice(image, corner_at, (2, WIN, WIN))
        return lax.dynamic_update_slice(image, current + grad_field[position], corner_at)
    return lax.fori_loop(0, grad_field.shape[0], add_one, jnp.zeros((2, OBJ, OBJ), jnp.float32))

def reference(object_slices, probes, measured, scan_offsets, probe_ids):
    table_real, table_imag = dft_tables(WIN)
    kernel_real, kernel_imag = kernel_table(WIN)
    start_wave = probes[probe_ids].astype(jnp.float32)

    def propagate(field_in, kernel_sign):
        spec_real, spec_imag = transform(field_in, table_real, table_imag)
        mixed_real, mixed_imag = complex_mul(spec_real, spec_imag, kernel_real, kernel_sign * kernel_imag)
        mixed_wave = jnp.stack([mixed_real, mixed_imag], 1)
        return transform(mixed_wave, table_real, -table_imag)

    def exit_of(wave_in, object_slab):
        windows = cut_windows(object_slab, scan_offsets).astype(jnp.float32)
        exit_real, exit_imag = complex_mul(wave_in[:, 0], wave_in[:, 1], windows[:, 0], windows[:, 1])
        return jnp.stack([exit_real, exit_imag], 1)

    def forward_slice(wave_in, object_slab):
        out_real, out_imag = propagate(exit_of(wave_in, object_slab), 1.0)
        return (jnp.stack([out_real, out_imag], 1), wave_in)
    unused_wave, stored = lax.scan(forward_slice, start_wave, object_slices)
    exit_last = exit_of(stored[NSLICE - 1], object_slices[NSLICE - 1])
    far_real, far_imag = transform(exit_last, table_real, table_imag)
    excess = far_real * far_real + far_imag * far_imag - measured
    residue = jnp.stack([excess * far_real, excess * far_imag], 1)
    seed_real, seed_imag = transform(residue, table_real, -table_imag)
    seed_wave = jnp.stack([seed_real, seed_imag], 1)

    def backward_slice(back_wave, inputs):
        object_slab, wave_in = inputs
        windows = cut_windows(object_slab, scan_offsets).astype(jnp.float32)
        term_real = wave_in[:, 0] * back_wave[:, 0] + wave_in[:, 1] * back_wave[:, 1]
        term_imag = wave_in[:, 0] * back_wave[:, 1] - wave_in[:, 1] * back_wave[:, 0]
        image = paint(jnp.stack([term_real, term_imag], 1), scan_offsets)
        sent_real = windows[:, 0] * back_wave[:, 0] + windows[:, 1] * back_wave[:, 1]
        sent_imag = windows[:, 0] * back_wave[:, 1] - windows[:, 1] * back_wave[:, 0]
        sent_wave = jnp.stack([sent_real, sent_imag], 1)
        prev_real, prev_imag = propagate(sent_wave, -1.0)
        return (jnp.stack([prev_real, prev_imag], 1), image)
    unused_back, images = lax.scan(backward_slice, seed_wave, (object_slices, stored), reverse=True)
    return images.astype(jnp.bfloat16)
```

```python
import functools
import math

import jax
import jax.numpy as jnp
import ml_dtypes
import numpy as np
from jax import lax
from jax.experimental import pallas as pl
from jax.experimental.pallas import tpu as pltpu
from jax.sharding import PartitionSpec as P

MESH = pl.DeviceIdType.MESH

PLAN = [[(0, 0), (6, 8)], [(0, 1), (6, 12)], [(0, 2), (6, 10)], [(0, 3), (6, 14)], [(0, 5), (8, 9)], [(0, 7), (8, 11)], [(0, 4)], [(0, 6)]]
HOLD = True
LATE = True


def split_table(table):
    high = table.astype(ml_dtypes.bfloat16)
    low = (table - high.astype(np.float64)).astype(ml_dtypes.bfloat16)
    return np.stack([high, low])


def right_left(matrix):
    real, imag = matrix.real, matrix.imag
    right = np.block([[real, imag], [-imag, real]])
    left = np.block([[real, -imag], [imag, real]])
    return np.stack([split_table(right), split_table(left)])


def tables(length):
    ordinal = np.arange(length)
    dft = np.exp(-2j * math.pi * (np.outer(ordinal, ordinal) % length) / length) / math.sqrt(length)
    spatial = np.where(ordinal < length // 2, ordinal, ordinal - length)
    chirp = np.exp(-1j * math.pi * (spatial * spatial % (2 * length)) / length)
    prop = (dft.conj() * chirp[None, :]) @ dft
    return np.stack([right_left(prop), right_left(dft)])


def split(values):
    high = values.astype(jnp.bfloat16)
    low = (values - high.astype(jnp.float32)).astype(jnp.bfloat16)
    return high, low


def dot(left, right):
    return jnp.dot(left, right, preferred_element_type=jnp.float32)


def two_sided(real, imag, table_ref, which):
    length = real.shape[0]
    high, low = split(jnp.concatenate([real, imag], axis=1))
    both = dot(jnp.concatenate([high, low], axis=0), table_ref[which, 0, 0])
    mid = both[:length] + both[length:] + dot(high, table_ref[which, 0, 1])
    stacked = jnp.concatenate([mid[:, :length], mid[:, length:]], axis=0)
    high, low = split(stacked)
    both = dot(table_ref[which, 1, 0], jnp.concatenate([high, low], axis=1))
    out = both[:, :length] + both[:, length:] + dot(table_ref[which, 1, 1], high)
    return out[:length], out[length:]


def complex_mul(left_real, left_imag, right_real, right_imag):
    return (
        left_real * right_real - left_imag * right_imag,
        left_real * right_imag + left_imag * right_real,
    )


def one_hot(length, width, start, axis):
    shape = (length, width) if axis == 0 else (width, length)
    place = lax.broadcasted_iota(jnp.int32, shape, axis)
    wanted = lax.broadcasted_iota(jnp.int32, shape, 1 - axis) + start
    return jnp.where(place == wanted, 1.0, 0.0).astype(jnp.bfloat16)


def plan(count, positions):
    if count == 2 * positions and positions == 8:
        return PLAN
    return [
        [(start, start + position) for start in range(0, count, positions)]
        for position in range(positions)
    ]


def tabulate(segments, count):
    positions = len(segments)
    roles = [(0, 0, 0, -1, -1)] * count
    where = [[None] * positions for _ in range(count)]
    for position, parts in enumerate(segments):
        ends = [start for start, _ in parts[1:]] + [count]
        for i, ((low, device), high) in enumerate(zip(parts, ends)):
            before = parts[i - 1][1] if i > 0 else -1
            after = parts[i + 1][1] if i + 1 < len(parts) else -1
            roles[device] = (position, low, high, before, after)
            for owner in range(low, high):
                where[owner][position] = (device, owner - low)
    orders = [send_order(segments, where, owner) for owner in range(count)]
    peers = [set() for _ in range(count)]
    for owner in range(count):
        for device, _ in where[owner]:
            if device != owner:
                peers[owner].add(device)
                peers[device].add(owner)
    for device, (_, low, high, before, after) in enumerate(roles):
        for other in (before, after):
            if other >= 0:
                peers[device].add(other)
                peers[other].add(device)
    orders, urgent = zip(*orders)
    return roles, where, orders, urgent, [sorted(p) for p in peers]


def send_order(segments, where, owner):
    count = len(where)

    def rank(position):
        device, _ = where[owner][position]
        if device // 2 == owner // 2:
            return (0, device != owner, 0, 0)
        late = (len(segments[position]) == 1) == (owner < count // 2) and LATE
        return (1 + late, 0, (device // 2 - owner // 2 - 1) % count, device)

    order = sorted(range(len(segments)), key=rank)
    return order, sum(rank(position)[0] < 2 for position in order)


def chain_kernel(
    segments, offsets, ids, obj_hbm, probes_hbm, measured_hbm, table_hbm,
    grads,
    table, obj, probes, measured, windows, win_in, waves, back_buf, grad_out, hop_out, hop_in,
    win_send, win_recv, grad_send, grad_recv, hop_send, hop_recv, load_sem,
):
    positions, window = measured_hbm.shape[0], measured_hbm.shape[-1]
    side = obj.shape[-1]
    me = lax.axis_index("depth")
    roles, where, orders, urgent, peers = segments
    count = len(roles)

    def look(values):
        found = jnp.int32(values[0])
        for device in range(1, count):
            if values[device] != values[device - 1]:
                found = jnp.where(me >= device, values[device], found)
        return found

    mine, low, high, before, after = (look([role[i] for role in roles]) for i in range(5))
    slots = high - low
    busy = slots > 0
    first = busy & (low == 0)
    final = high == count

    loads = [
        pltpu.make_async_copy(source, target, load_sem.at[i])
        for i, (source, target) in enumerate((
            (obj_hbm.at[0], obj), (table_hbm, table), (probes_hbm, probes),
            (measured_hbm.at[mine], measured),
        ))
    ]
    for load in loads:
        load.start()

    barrier = pltpu.get_barrier_semaphore()
    most = max(len(p) for p in peers)
    for i in range(most):
        peer = look([p[i] if i < len(p) else -1 for p in peers])

        @pl.when(peer >= 0)
        def _():
            pl.semaphore_signal(
                barrier, inc=1, device_id={"depth": peer}, device_id_type=MESH
            )

    greetings = look([len(p) for p in peers])
    ahead = look(urgent)

    turns = []
    for turn in range(positions):
        packed = [
            (orders[d][turn] * count + where[d][orders[d][turn]][0]) * count
            + where[d][orders[d][turn]][1]
            for d in range(count)
        ]
        code = look(packed)
        turns.append((code // (count * count), code // count % count, code % count))

    def win_copy(place, device, slot):
        return pltpu.make_async_remote_copy(
            src_ref=windows.at[place], dst_ref=win_in.at[slot],
            send_sem=win_send.at[place], recv_sem=win_recv.at[slot],
            device_id={"depth": device}, device_id_type=MESH,
        )

    def cut(places):
        across = [one_hot(side, window, offsets[1, place], 0) for place in places]
        strips = dot(field, jnp.concatenate(across, axis=1)).astype(jnp.bfloat16)
        for i, place in enumerate(places):
            strip = strips[:, i * window : (i + 1) * window]
            strip = jnp.concatenate([strip[:side], strip[side:]], axis=1)
            tile = dot(one_hot(side, window, offsets[0, place], 1), strip)
            windows[place, 0] = tile[:, :window]
            windows[place, 1] = tile[:, window:]

    def ship(place, device, slot):
        @pl.when(device != me)
        def _():
            win_copy(place, device, slot).start()

        @pl.when(device == me)
        def _():
            win_in[slot] = windows[place]

    def shipped(place, device, slot):
        @pl.when(device != me)
        def _():
            win_copy(place, device, slot).wait_send()

    loads[0].wait()
    field = obj[...].reshape(2 * side, side)
    for turn in range(0, positions, 2):
        cut([turns[turn][0], turns[turn + 1][0]])
        if turn == 0:
            pl.semaphore_wait(barrier, greetings)
        for near in (turn, turn + 1):
            @pl.when(near < ahead)
            def _():
                ship(*turns[near])

    for turn, target in enumerate(turns):
        @pl.when(turn < ahead)
        def _():
            shipped(*target)

    def ship_rest():
        for turn, target in enumerate(turns):
            @pl.when(turn >= ahead)
            def _():
                ship(*target)

    held = busy & (low == 0) & jnp.logical_not(final) if HOLD else jnp.bool_(False)

    @pl.when(jnp.logical_not(held))
    def _():
        ship_rest()

    for load in loads[1:]:
        load.wait()

    def hop(which, peer):
        return pltpu.make_async_remote_copy(
            src_ref=hop_out.at[which], dst_ref=hop_in.at[which],
            send_sem=hop_send.at[which], recv_sem=hop_recv.at[which],
            device_id={"depth": peer}, device_id_type=MESH,
        )

    @pl.when(first)
    def _():
        chosen = ids[mine]
        wave = jnp.zeros(probes.shape[1:], jnp.float32)
        for which in range(probes.shape[0]):
            wave = jnp.where(chosen == which, probes[which], wave)
        waves[0] = wave

    def win_wait(slot):
        @pl.when(low + slot != me)
        def _():
            pltpu.make_async_remote_copy(
                src_ref=windows.at[0], dst_ref=win_in.at[slot],
                send_sem=win_send.at[0], recv_sem=win_recv.at[slot],
                device_id={"depth": low + slot}, device_id_type=MESH,
            ).wait_recv()

    def exit_wave(slot):
        return complex_mul(waves[slot, 0], waves[slot, 1], win_in[slot, 0], win_in[slot, 1])

    def advance(slot):
        real, imag = two_sided(*exit_wave(slot), table, 0)
        waves[slot + 1, 0] = real
        waves[slot + 1, 1] = imag

    def forward(pair, carry):
        win_wait(2 * pair + 1)
        win_wait(2 * pair + 2)
        advance(2 * pair + 1)
        advance(2 * pair + 2)
        return carry

    def grad_copy(slot):
        return pltpu.make_async_remote_copy(
            src_ref=grad_out.at[slot], dst_ref=grads.at[mine],
            send_sem=grad_send.at[slot], recv_sem=grad_recv.at[mine],
            device_id={"depth": low + slot}, device_id_type=MESH,
        )

    def keep_copy(slot):
        return pltpu.make_async_copy(grad_out.at[slot], grads.at[mine], load_sem.at[0])

    def keep_term(slot):
        real, imag = complex_mul(waves[slot, 0], waves[slot, 1], back_buf[0], back_buf[1])
        grad_out[slot, 0] = real
        grad_out[slot, 1] = -imag

    def give(slot):
        @pl.when(low + slot == me)
        def _():
            keep_copy(slot).start()

        @pl.when((low + slot != me) & (low == 0))
        def _():
            grad_copy(slot).start()

    def send_back(slot):
        return two_sided(
            *complex_mul(win_in[slot, 0], win_in[slot, 1], back_buf[0], back_buf[1]), table, 0
        )

    def retreat(slot):
        keep_term(slot)
        real, imag = send_back(slot)
        back_buf[0] = real
        back_buf[1] = imag
        give(slot)

    def backward(pair, carry):
        retreat(slots - 2 - 2 * pair)
        retreat(slots - 3 - 2 * pair)
        return carry

    @pl.when(busy)
    def _():
        @pl.when(low > 0)
        def _():
            hop(0, before).wait_recv()
            waves[0] = hop_in[0]

        win_wait(0)
        advance(0)
        lax.fori_loop(0, slots // 2 - 1, forward, 0)
        win_wait(slots - 1)

        @pl.when(jnp.logical_not(final))
        def _():
            real, imag = two_sided(*exit_wave(slots - 1), table, 0)
            hop_out[0, 0] = real
            hop_out[0, 1] = imag
            hop(0, after).start()

            @pl.when(held)
            def _():
                ship_rest()

            hop(1, after).wait_recv()
            back_buf[0] = hop_in[1, 0]
            back_buf[1] = hop_in[1, 1]

        @pl.when(final)
        def _():
            far_real, far_imag = two_sided(*exit_wave(slots - 1), table, 1)
            excess = far_real * far_real + far_imag * far_imag - measured[...]
            real, imag = two_sided(excess * far_real, -(excess * far_imag), table, 1)
            back_buf[0] = real
            back_buf[1] = imag

        retreat(slots - 1)
        lax.fori_loop(0, slots // 2 - 1, backward, 0)

        @pl.when(low > 0)
        def _():
            real, imag = send_back(0)
            hop_out[1, 0] = real
            hop_out[1, 1] = imag
            hop(1, before).start()

        keep_term(0)
        give(0)

        @pl.when(low > 0)
        def _():
            def late(step, carry):
                slot = slots - 1 - step

                @pl.when(low + slot != me)
                def _():
                    grad_copy(slot).start()

                return carry

            lax.fori_loop(0, slots, late, 0)
            hop(1, before).wait_send()

        @pl.when(jnp.logical_not(final))
        def _():
            hop(0, after).wait_send()

        def sent(slot, carry):
            @pl.when(low + slot != me)
            def _():
                grad_copy(slot).wait_send()

            @pl.when(low + slot == me)
            def _():
                keep_copy(slot).wait()

            return carry

        lax.fori_loop(0, slots, sent, 0)

    for turn, target in enumerate(turns):
        @pl.when(turn >= ahead)
        def _():
            shipped(*target)

    for place, device, slot in turns:
        @pl.when(device != me)
        def _():
            pltpu.make_async_remote_copy(
                src_ref=grad_out.at[0], dst_ref=grads.at[place],
                send_sem=grad_send.at[0], recv_sem=grad_recv.at[place],
                device_id={"depth": device}, device_id_type=MESH,
            ).wait_recv()


def paint_kernel(offsets, grads, out_hbm, out, total, store_sem):
    positions, window = grads.shape[0], grads.shape[-1]
    side = out.shape[-1]
    total[...] = jnp.zeros_like(total)
    tall, wide = window + 8, 2 * window
    for position in range(positions):
        row, col = offsets[0, position], offsets[1, position]
        row_base = jnp.minimum((row >> 3) << 3, side - tall)
        col_base = jnp.minimum(col // window * window, side - wide)
        rows = pl.ds(pl.multiple_of(row_base, 8), tall)
        cols = pl.ds(pl.multiple_of(col_base, 128), wide)
        for part in range(2):
            tile = grads[position, part]
            tile = jnp.concatenate([tile, jnp.zeros((8, window), jnp.float32)], axis=0)
            tile = pltpu.roll(tile, row - row_base, 0)
            tile = jnp.concatenate([tile, jnp.zeros((tall, window), jnp.float32)], axis=1)
            tile = pltpu.roll(tile, col - col_base, 1)
            total[part, rows, cols] += tile
    pieces = store_sem.shape[0]
    tall = side // pieces
    stores = []
    for piece in range(pieces):
        rows = pl.ds(piece * tall, tall)
        out[:, rows] = total[:, rows].astype(out.dtype)
        stores.append(
            pltpu.make_async_copy(out.at[:, rows], out_hbm.at[0, :, rows], store_sem.at[piece])
        )
        stores[-1].start()
    for store in stores:
        store.wait()


def body(object_slices, probes, measured, scan_offsets, probe_ids, *, count):
    positions, window = measured.shape[0], measured.shape[-1]
    side = object_slices.shape[-1]
    assert count % positions == 0 and positions % 8 == 0
    table = jnp.asarray(tables(window))
    smem = pl.BlockSpec(memory_space=pltpu.SMEM)
    vmem = pl.BlockSpec(memory_space=pltpu.VMEM)
    field = (2, window, window)
    segments = tabulate(plan(count, positions), count)
    longest = max(high - low for _, low, high, _, _ in segments[0])
    stack = pltpu.VMEM((positions,) + field, jnp.float32)
    chain = pltpu.VMEM((longest,) + field, jnp.float32)
    sems = pltpu.SemaphoreType.DMA((positions,))
    chain_sems = pltpu.SemaphoreType.DMA((longest,))
    hbm = pl.BlockSpec(memory_space=pltpu.HBM)
    grads = pl.pallas_call(
        functools.partial(chain_kernel, segments),
        out_shape=pltpu.VMEM((positions,) + field, jnp.float32),
        in_specs=[smem, smem, hbm, hbm, hbm, hbm],
        out_specs=vmem,
        scratch_shapes=[
            pltpu.VMEM(table.shape, jnp.bfloat16),
            pltpu.VMEM(object_slices.shape[1:], jnp.bfloat16),
            pltpu.VMEM(probes.shape, jnp.float32),
            pltpu.VMEM((window, window), jnp.float32),
            stack, chain, chain,
            pltpu.VMEM(field, jnp.float32),
            chain,
            pltpu.VMEM((2,) + field, jnp.float32),
            pltpu.VMEM((2,) + field, jnp.float32),
            sems, chain_sems, chain_sems, sems,
            pltpu.SemaphoreType.DMA((2,)),
            pltpu.SemaphoreType.DMA((2,)),
            pltpu.SemaphoreType.DMA((4,)),
        ],
        compiler_params=pltpu.CompilerParams(
            collective_id=0, has_side_effects=True, vmem_limit_bytes=58 * 1024 * 1024
        ),
    )(scan_offsets.T, probe_ids, object_slices, probes, measured, table)
    return pl.pallas_call(
        paint_kernel,
        out_shape=jax.ShapeDtypeStruct(object_slices.shape, jnp.bfloat16),
        in_specs=[smem, vmem],
        out_specs=hbm,
        scratch_shapes=[
            pltpu.VMEM((2, side, side), jnp.bfloat16),
            pltpu.VMEM((2, side, side), jnp.float32),
            pltpu.SemaphoreType.DMA((4,)),
        ],
        compiler_params=pltpu.CompilerParams(vmem_limit_bytes=32 * 1024 * 1024),
    )(scan_offsets.T, grads)


def solution(mesh):
    return jax.shard_map(
        functools.partial(body, count=mesh.shape["depth"]),
        mesh=mesh,
        in_specs=(
            P(("groups", "depth"), None, None, None),
            P("groups", None, None, None),
            P("groups", None, None),
            P("groups", None),
            P("groups"),
        ),
        out_specs=P(("groups", "depth"), None, None, None),
        check_vma=False,
    )
```

```python
import functools
import math

import jax
import jax.numpy as jnp
import ml_dtypes
import numpy as np
from jax import lax
from jax.experimental import pallas as pl
from jax.experimental.pallas import tpu as pltpu
from jax.sharding import PartitionSpec as P

MESH = pl.DeviceIdType.MESH

PLAN = [[(0, 7)], [(0, 1), (6, 15)], [(0, 5)], [(0, 6), (4, 9)], [(0, 0), (8, 12)], [(0, 3), (4, 11)], [(0, 2), (6, 10)], [(0, 4)]]
RANKS = [[0, 2], [1, 0], [1, 1], [0, 1], [0, 2], [0, 3], [0, 0], [3, 1]]


def split_table(table):
    high = table.astype(ml_dtypes.bfloat16)
    low = (table - high.astype(np.float64)).astype(ml_dtypes.bfloat16)
    return np.stack([high, low])


def right_left(matrix):
    real, imag = matrix.real, matrix.imag
    right = np.block([[real, imag], [-imag, real]])
    left = np.block([[real, -imag], [imag, real]])
    return np.stack([split_table(right), split_table(left)])


def tables(length):
    ordinal = np.arange(length)
    dft = np.exp(-2j * math.pi * (np.outer(ordinal, ordinal) % length) / length) / math.sqrt(length)
    spatial = np.where(ordinal < length // 2, ordinal, ordinal - length)
    chirp = np.exp(-1j * math.pi * (spatial * spatial % (2 * length)) / length)
    prop = (dft.conj() * chirp[None, :]) @ dft
    return np.stack([right_left(prop), right_left(dft)])


def split(values):
    high = values.astype(jnp.bfloat16)
    low = (values - high.astype(jnp.float32)).astype(jnp.bfloat16)
    return high, low


def dot(left, right):
    return jnp.dot(left, right, preferred_element_type=jnp.float32)


def two_sided(real, imag, table_ref, which):
    length = real.shape[0]
    high, low = split(jnp.concatenate([real, imag], axis=1))
    both = dot(jnp.concatenate([high, low], axis=0), table_ref[which, 0, 0])
    mid = both[:length] + both[length:] + dot(high, table_ref[which, 0, 1])
    stacked = jnp.concatenate([mid[:, :length], mid[:, length:]], axis=0)
    high, low = split(stacked)
    both = dot(table_ref[which, 1, 0], jnp.concatenate([high, low], axis=1))
    out = both[:, :length] + both[:, length:] + dot(table_ref[which, 1, 1], high)
    return out[:length], out[length:]


def complex_mul(left_real, left_imag, right_real, right_imag):
    return (
        left_real * right_real - left_imag * right_imag,
        left_real * right_imag + left_imag * right_real,
    )


def one_hot(length, width, start, axis):
    shape = (length, width) if axis == 0 else (width, length)
    place = lax.broadcasted_iota(jnp.int32, shape, axis)
    wanted = lax.broadcasted_iota(jnp.int32, shape, 1 - axis) + start
    return jnp.where(place == wanted, 1.0, 0.0).astype(jnp.bfloat16)


def tuned(count, positions):
    return count == 16 and positions == 8


def plan(count, positions):
    if tuned(count, positions):
        return PLAN
    return [
        [(start, start + position) for start in range(0, count, positions)]
        for position in range(positions)
    ]


def tabulate(segments, count):
    positions = len(segments)
    roles = [(0, 0, 0, -1, -1)] * count
    where = [[None] * positions for _ in range(count)]
    for position, parts in enumerate(segments):
        ends = [start for start, _ in parts[1:]] + [count]
        for i, ((low, device), high) in enumerate(zip(parts, ends)):
            before = parts[i - 1][1] if i > 0 else -1
            after = parts[i + 1][1] if i + 1 < len(parts) else -1
            roles[device] = (position, low, high, before, after)
            for owner in range(low, high):
                where[owner][position] = (device, owner - low)
    orders = [send_order(segments, where, roles, owner) for owner in range(count)]
    peers = [set() for _ in range(count)]
    for owner in range(count):
        for device, _ in where[owner]:
            if device != owner:
                peers[owner].add(device)
                peers[device].add(owner)
    for device, (_, low, high, before, after) in enumerate(roles):
        for other in (before, after):
            if other >= 0:
                peers[device].add(other)
                peers[other].add(device)
    orders, urgent = zip(*orders)
    return roles, where, orders, urgent, [sorted(p) for p in peers]


def send_order(segments, where, roles, owner):
    count = len(where)

    def rank(position):
        device, _ = where[owner][position]
        parts = [i for i, (_, held) in enumerate(segments[position]) if held == device]
        if device // 2 == owner // 2:
            return (0, device != owner, 0, 0)
        return (RANKS[position][parts[0]] if tuned(count, len(segments)) else 0, 1, (device // 2 - owner // 2 - 1) % count, device)

    order = sorted(range(len(segments)), key=rank)
    _, low, high, _, _ = roles[owner]
    if low == 0 and 0 < high < count:
        return order, sum(rank(position)[0] < 2 for position in order)
    return order, len(order)


def chain_kernel(
    segments, offsets, ids, obj_hbm, probes_hbm, measured_hbm, table_hbm,
    grads,
    table, obj, probes, measured, windows, win_in, waves, back_buf, grad_out, hop_out, hop_in,
    win_send, win_recv, grad_send, grad_recv, hop_send, hop_recv, load_sem,
):
    positions, window = measured_hbm.shape[0], measured_hbm.shape[-1]
    side = obj.shape[-1]
    me = lax.axis_index("depth")
    roles, where, orders, urgent, peers = segments
    count = len(roles)

    def look(values):
        found = jnp.int32(values[0])
        for device in range(1, count):
            if values[device] != values[device - 1]:
                found = jnp.where(me >= device, values[device], found)
        return found

    mine, low, high, before, after = (look([role[i] for role in roles]) for i in range(5))
    slots = high - low
    busy = slots > 0
    first = busy & (low == 0)
    final = high == count

    loads = [
        pltpu.make_async_copy(source, target, load_sem.at[i])
        for i, (source, target) in enumerate((
            (obj_hbm.at[0], obj), (table_hbm, table), (probes_hbm, probes),
            (measured_hbm.at[mine], measured),
        ))
    ]
    for load in loads:
        load.start()

    barrier = pltpu.get_barrier_semaphore()
    most = max(len(p) for p in peers)
    for i in range(most):
        peer = look([p[i] if i < len(p) else -1 for p in peers])

        @pl.when(peer >= 0)
        def _():
            pl.semaphore_signal(
                barrier, inc=1, device_id={"depth": peer}, device_id_type=MESH
            )

    greetings = look([len(p) for p in peers])
    ahead = look(urgent)

    turns = []
    for turn in range(positions):
        packed = [
            (orders[d][turn] * count + where[d][orders[d][turn]][0]) * count
            + where[d][orders[d][turn]][1]
            for d in range(count)
        ]
        code = look(packed)
        turns.append((code // (count * count), code // count % count, code % count))

    def win_copy(place, device, slot):
        return pltpu.make_async_remote_copy(
            src_ref=windows.at[place], dst_ref=win_in.at[slot],
            send_sem=win_send.at[place], recv_sem=win_recv.at[slot],
            device_id={"depth": device}, device_id_type=MESH,
        )

    def cut(places):
        across = [one_hot(side, window, offsets[1, place], 0) for place in places]
        strips = dot(field, jnp.concatenate(across, axis=1)).astype(jnp.bfloat16)
        for i, place in enumerate(places):
            strip = strips[:, i * window : (i + 1) * window]
            strip = jnp.concatenate([strip[:side], strip[side:]], axis=1)
            tile = dot(one_hot(side, window, offsets[0, place], 1), strip)
            windows[place, 0] = tile[:, :window]
            windows[place, 1] = tile[:, window:]

    def ship(place, device, slot):
        @pl.when(device != me)
        def _():
            win_copy(place, device, slot).start()

        @pl.when(device == me)
        def _():
            win_in[slot] = windows[place]

    def shipped(place, device, slot):
        @pl.when(device != me)
        def _():
            win_copy(place, device, slot).wait_send()

    loads[0].wait()
    field = obj[...].reshape(2 * side, side)
    for turn in range(0, positions, 2):
        cut([turns[turn][0], turns[turn + 1][0]])
        if turn == 0:
            pl.semaphore_wait(barrier, greetings)
        for near in (turn, turn + 1):
            @pl.when(near < ahead)
            def _():
                ship(*turns[near])

    def ship_rest():
        for turn, target in enumerate(turns):
            @pl.when(turn >= ahead)
            def _():
                ship(*target)

    for load in loads[1:]:
        load.wait()

    def hop(which, peer):
        return pltpu.make_async_remote_copy(
            src_ref=hop_out.at[which], dst_ref=hop_in.at[which],
            send_sem=hop_send.at[which], recv_sem=hop_recv.at[which],
            device_id={"depth": peer}, device_id_type=MESH,
        )

    @pl.when(first)
    def _():
        chosen = ids[mine]
        wave = jnp.zeros(probes.shape[1:], jnp.float32)
        for which in range(probes.shape[0]):
            wave = jnp.where(chosen == which, probes[which], wave)
        waves[0] = wave

    def win_wait(slot):
        @pl.when(low + slot != me)
        def _():
            pltpu.make_async_remote_copy(
                src_ref=windows.at[0], dst_ref=win_in.at[slot],
                send_sem=win_send.at[0], recv_sem=win_recv.at[slot],
                device_id={"depth": low + slot}, device_id_type=MESH,
            ).wait_recv()

    def exit_wave(slot):
        return complex_mul(waves[slot, 0], waves[slot, 1], win_in[slot, 0], win_in[slot, 1])

    def advance(slot):
        real, imag = two_sided(*exit_wave(slot), table, 0)
        waves[slot + 1, 0] = real
        waves[slot + 1, 1] = imag

    def forward(pair, carry):
        win_wait(2 * pair + 1)
        win_wait(2 * pair + 2)
        advance(2 * pair + 1)
        advance(2 * pair + 2)
        return carry

    def grad_copy(slot):
        return pltpu.make_async_remote_copy(
            src_ref=grad_out.at[slot], dst_ref=grads.at[mine],
            send_sem=grad_send.at[slot], recv_sem=grad_recv.at[mine],
            device_id={"depth": low + slot}, device_id_type=MESH,
        )

    def keep_copy(slot):
        return pltpu.make_async_copy(grad_out.at[slot], grads.at[mine], load_sem.at[0])

    def keep_term(slot):
        real, imag = complex_mul(waves[slot, 0], waves[slot, 1], back_buf[0], back_buf[1])
        grad_out[slot, 0] = real
        grad_out[slot, 1] = -imag

    def give(slot):
        @pl.when(low + slot == me)
        def _():
            keep_copy(slot).start()

        @pl.when((low + slot != me) & (low == 0))
        def _():
            grad_copy(slot).start()

    def send_back(slot):
        return two_sided(
            *complex_mul(win_in[slot, 0], win_in[slot, 1], back_buf[0], back_buf[1]), table, 0
        )

    def retreat(slot):
        keep_term(slot)
        real, imag = send_back(slot)
        back_buf[0] = real
        back_buf[1] = imag
        give(slot)

    def backward(pair, carry):
        retreat(slots - 2 - 2 * pair)
        retreat(slots - 3 - 2 * pair)
        return carry

    @pl.when(busy)
    def _():
        @pl.when(low > 0)
        def _():
            hop(0, before).wait_recv()
            waves[0] = hop_in[0]

        win_wait(0)
        advance(0)
        lax.fori_loop(0, slots // 2 - 1, forward, 0)
        win_wait(slots - 1)

        @pl.when(jnp.logical_not(final))
        def _():
            real, imag = two_sided(*exit_wave(slots - 1), table, 0)
            hop_out[0, 0] = real
            hop_out[0, 1] = imag
            hop(0, after).start()

            ship_rest()
            hop(1, after).wait_recv()
            back_buf[0] = hop_in[1, 0]
            back_buf[1] = hop_in[1, 1]

        @pl.when(final)
        def _():
            far_real, far_imag = two_sided(*exit_wave(slots - 1), table, 1)
            excess = far_real * far_real + far_imag * far_imag - measured[...]
            real, imag = two_sided(excess * far_real, -(excess * far_imag), table, 1)
            back_buf[0] = real
            back_buf[1] = imag

        retreat(slots - 1)
        lax.fori_loop(0, slots // 2 - 1, backward, 0)

        @pl.when(low > 0)
        def _():
            real, imag = send_back(0)
            hop_out[1, 0] = real
            hop_out[1, 1] = imag
            hop(1, before).start()

        keep_term(0)
        give(0)

        @pl.when(low > 0)
        def _():
            def late(step, carry):
                slot = slots - 1 - step

                @pl.when(low + slot != me)
                def _():
                    grad_copy(slot).start()

                return carry

            lax.fori_loop(0, slots, late, 0)
            hop(1, before).wait_send()

        @pl.when(jnp.logical_not(final))
        def _():
            hop(0, after).wait_send()

        def sent(slot, carry):
            @pl.when(low + slot != me)
            def _():
                grad_copy(slot).wait_send()

            @pl.when(low + slot == me)
            def _():
                keep_copy(slot).wait()

            return carry

        lax.fori_loop(0, slots, sent, 0)

    for target in turns:
        shipped(*target)

    for place, device, slot in turns:
        @pl.when(device != me)
        def _():
            pltpu.make_async_remote_copy(
                src_ref=grad_out.at[0], dst_ref=grads.at[place],
                send_sem=grad_send.at[0], recv_sem=grad_recv.at[place],
                device_id={"depth": device}, device_id_type=MESH,
            ).wait_recv()


def paint_kernel(offsets, grads, out_hbm, out, total, store_sem):
    positions, window = grads.shape[0], grads.shape[-1]
    side = out.shape[-1]
    total[...] = jnp.zeros_like(total)
    tall, wide = window + 8, 2 * window
    for position in range(positions):
        row, col = offsets[0, position], offsets[1, position]
        row_base = jnp.minimum((row >> 3) << 3, side - tall)
        col_base = jnp.minimum(col // window * window, side - wide)
        rows = pl.ds(pl.multiple_of(row_base, 8), tall)
        cols = pl.ds(pl.multiple_of(col_base, 128), wide)
        for part in range(2):
            tile = grads[position, part]
            tile = jnp.concatenate([tile, jnp.zeros((8, window), jnp.float32)], axis=0)
            tile = pltpu.roll(tile, row - row_base, 0)
            tile = jnp.concatenate([tile, jnp.zeros((tall, window), jnp.float32)], axis=1)
            tile = pltpu.roll(tile, col - col_base, 1)
            total[part, rows, cols] += tile
    pieces = store_sem.shape[0]
    tall = side // pieces
    stores = []
    for piece in range(pieces):
        rows = pl.ds(piece * tall, tall)
        out[:, rows] = total[:, rows].astype(out.dtype)
        stores.append(
            pltpu.make_async_copy(out.at[:, rows], out_hbm.at[0, :, rows], store_sem.at[piece])
        )
        stores[-1].start()
    for store in stores:
        store.wait()


def body(object_slices, probes, measured, scan_offsets, probe_ids, *, count):
    positions, window = measured.shape[0], measured.shape[-1]
    side = object_slices.shape[-1]
    assert count % positions == 0 and positions % 8 == 0
    table = jnp.asarray(tables(window))
    smem = pl.BlockSpec(memory_space=pltpu.SMEM)
    vmem = pl.BlockSpec(memory_space=pltpu.VMEM)
    field = (2, window, window)
    segments = tabulate(plan(count, positions), count)
    longest = max(high - low for _, low, high, _, _ in segments[0])
    stack = pltpu.VMEM((positions,) + field, jnp.float32)
    chain = pltpu.VMEM((longest,) + field, jnp.float32)
    sems = pltpu.SemaphoreType.DMA((positions,))
    chain_sems = pltpu.SemaphoreType.DMA((longest,))
    hbm = pl.BlockSpec(memory_space=pltpu.HBM)
    grads = pl.pallas_call(
        functools.partial(chain_kernel, segments),
        out_shape=pltpu.VMEM((positions,) + field, jnp.float32),
        in_specs=[smem, smem, hbm, hbm, hbm, hbm],
        out_specs=vmem,
        scratch_shapes=[
            pltpu.VMEM(table.shape, jnp.bfloat16),
            pltpu.VMEM(object_slices.shape[1:], jnp.bfloat16),
            pltpu.VMEM(probes.shape, jnp.float32),
            pltpu.VMEM((window, window), jnp.float32),
            stack, chain, chain,
            pltpu.VMEM(field, jnp.float32),
            chain,
            pltpu.VMEM((2,) + field, jnp.float32),
            pltpu.VMEM((2,) + field, jnp.float32),
            sems, chain_sems, chain_sems, sems,
            pltpu.SemaphoreType.DMA((2,)),
            pltpu.SemaphoreType.DMA((2,)),
            pltpu.SemaphoreType.DMA((4,)),
        ],
        compiler_params=pltpu.CompilerParams(
            collective_id=0, has_side_effects=True, vmem_limit_bytes=58 * 1024 * 1024
        ),
    )(scan_offsets.T, probe_ids, object_slices, probes, measured, table)
    return pl.pallas_call(
        paint_kernel,
        out_shape=jax.ShapeDtypeStruct(object_slices.shape, jnp.bfloat16),
        in_specs=[smem, vmem],
        out_specs=hbm,
        scratch_shapes=[
            pltpu.VMEM((2, side, side), jnp.bfloat16),
            pltpu.VMEM((2, side, side), jnp.float32),
            pltpu.SemaphoreType.DMA((4,)),
        ],
        compiler_params=pltpu.CompilerParams(vmem_limit_bytes=32 * 1024 * 1024),
    )(scan_offsets.T, grads)


def solution(mesh):
    return jax.shard_map(
        functools.partial(body, count=mesh.shape["depth"]),
        mesh=mesh,
        in_specs=(
            P(("groups", "depth"), None, None, None),
            P("groups", None, None, None),
            P("groups", None, None),
            P("groups", None),
            P("groups"),
        ),
        out_specs=P(("groups", "depth"), None, None, None),
        check_vma=False,
    )
```

```python
import functools
import math

import jax
import jax.numpy as jnp
import ml_dtypes
import numpy as np
from jax import lax
from jax.experimental import pallas as pl
from jax.experimental.pallas import tpu as pltpu
from jax.sharding import PartitionSpec as P

MESH = pl.DeviceIdType.MESH

PLAN = [[(0, 5)], [(0, 0), (6, 15)], [(0, 7)], [(0, 3), (4, 8)], [(0, 1), (8, 12)], [(0, 6), (4, 10)], [(0, 2), (6, 11)], [(0, 4)]]
RANKS = [[0, 2], [1, 1], [0, 1], [0, 1], [0, 1], [0, 3], [0, 0], [3, 1]]


def split_table(table):
    high = table.astype(ml_dtypes.bfloat16)
    low = (table - high.astype(np.float64)).astype(ml_dtypes.bfloat16)
    return np.stack([high, low])


def right_left(matrix):
    real, imag = matrix.real, matrix.imag
    right = np.block([[real, imag], [-imag, real]])
    left = np.block([[real, -imag], [imag, real]])
    return np.stack([split_table(right), split_table(left)])


def tables(length):
    ordinal = np.arange(length)
    dft = np.exp(-2j * math.pi * (np.outer(ordinal, ordinal) % length) / length) / math.sqrt(length)
    spatial = np.where(ordinal < length // 2, ordinal, ordinal - length)
    chirp = np.exp(-1j * math.pi * (spatial * spatial % (2 * length)) / length)
    prop = (dft.conj() * chirp[None, :]) @ dft
    return np.stack([right_left(prop), right_left(dft)])


def split(values):
    high = values.astype(jnp.bfloat16)
    low = (values - high.astype(jnp.float32)).astype(jnp.bfloat16)
    return high, low


def dot(left, right):
    return jnp.dot(left, right, preferred_element_type=jnp.float32)


def two_sided(real, imag, table_ref, which):
    length = real.shape[0]
    high, low = split(jnp.concatenate([real, imag], axis=1))
    both = dot(jnp.concatenate([high, low], axis=0), table_ref[which, 0, 0])
    mid = both[:length] + both[length:] + dot(high, table_ref[which, 0, 1])
    stacked = jnp.concatenate([mid[:, :length], mid[:, length:]], axis=0)
    high, low = split(stacked)
    both = dot(table_ref[which, 1, 0], jnp.concatenate([high, low], axis=1))
    out = both[:, :length] + both[:, length:] + dot(table_ref[which, 1, 1], high)
    return out[:length], out[length:]


def complex_mul(left_real, left_imag, right_real, right_imag):
    return (
        left_real * right_real - left_imag * right_imag,
        left_real * right_imag + left_imag * right_real,
    )


def one_hot(length, width, start, axis):
    shape = (length, width) if axis == 0 else (width, length)
    place = lax.broadcasted_iota(jnp.int32, shape, axis)
    wanted = lax.broadcasted_iota(jnp.int32, shape, 1 - axis) + start
    return jnp.where(place == wanted, 1.0, 0.0).astype(jnp.bfloat16)


def tuned(count, positions):
    return count == 16 and positions == 8


def plan(count, positions):
    if tuned(count, positions):
        return PLAN
    return [
        [(start, start + position) for start in range(0, count, positions)]
        for position in range(positions)
    ]


def tabulate(segments, count):
    positions = len(segments)
    roles = [(0, 0, 0, -1, -1)] * count
    where = [[None] * positions for _ in range(count)]
    for position, parts in enumerate(segments):
        ends = [start for start, _ in parts[1:]] + [count]
        for i, ((low, device), high) in enumerate(zip(parts, ends)):
            before = parts[i - 1][1] if i > 0 else -1
            after = parts[i + 1][1] if i + 1 < len(parts) else -1
            roles[device] = (position, low, high, before, after)
            for owner in range(low, high):
                where[owner][position] = (device, owner - low)
    orders = [send_order(segments, where, roles, owner) for owner in range(count)]
    peers = [set() for _ in range(count)]
    for owner in range(count):
        for device, _ in where[owner]:
            if device != owner:
                peers[owner].add(device)
                peers[device].add(owner)
    for device, (_, low, high, before, after) in enumerate(roles):
        for other in (before, after):
            if other >= 0:
                peers[device].add(other)
                peers[other].add(device)
    orders, urgent = zip(*orders)
    return roles, where, orders, urgent, [sorted(p) for p in peers]


def send_order(segments, where, roles, owner):
    count = len(where)

    def rank(position):
        device, _ = where[owner][position]
        parts = [i for i, (_, held) in enumerate(segments[position]) if held == device]
        if device // 2 == owner // 2:
            return (0, device != owner, 0, 0)
        return (RANKS[position][parts[0]] if tuned(count, len(segments)) else 0, 1, (device // 2 - owner // 2 - 1) % count, device)

    order = sorted(range(len(segments)), key=rank)
    _, low, high, _, _ = roles[owner]
    if low == 0 and 0 < high < count:
        return order, sum(rank(position)[0] < 2 for position in order)
    return order, len(order)


def chain_kernel(
    segments, offsets, ids, obj_hbm, probes_hbm, measured_hbm, table_hbm,
    grads,
    table, obj, probes, measured, windows, win_in, waves, back_buf, grad_out, hop_out, hop_in,
    win_send, win_recv, grad_send, grad_recv, hop_send, hop_recv, load_sem,
):
    positions, window = measured_hbm.shape[0], measured_hbm.shape[-1]
    side = obj.shape[-1]
    me = lax.axis_index("depth")
    roles, where, orders, urgent, peers = segments
    count = len(roles)

    def look(values):
        found = jnp.int32(values[0])
        for device in range(1, count):
            if values[device] != values[device - 1]:
                found = jnp.where(me >= device, values[device], found)
        return found

    mine, low, high, before, after = (look([role[i] for role in roles]) for i in range(5))
    slots = high - low
    busy = slots > 0
    first = busy & (low == 0)
    final = high == count

    loads = [
        pltpu.make_async_copy(source, target, load_sem.at[i])
        for i, (source, target) in enumerate((
            (obj_hbm.at[0], obj), (table_hbm, table), (probes_hbm, probes),
            (measured_hbm.at[mine], measured),
        ))
    ]
    for load in loads:
        load.start()

    barrier = pltpu.get_barrier_semaphore()
    most = max(len(p) for p in peers)
    for i in range(most):
        peer = look([p[i] if i < len(p) else -1 for p in peers])

        @pl.when(peer >= 0)
        def _():
            pl.semaphore_signal(
                barrier, inc=1, device_id={"depth": peer}, device_id_type=MESH
            )

    greetings = look([len(p) for p in peers])
    ahead = look(urgent)

    turns = []
    for turn in range(positions):
        packed = [
            (orders[d][turn] * count + where[d][orders[d][turn]][0]) * count
            + where[d][orders[d][turn]][1]
            for d in range(count)
        ]
        code = look(packed)
        turns.append((code // (count * count), code // count % count, code % count))

    def win_copy(place, device, slot):
        return pltpu.make_async_remote_copy(
            src_ref=windows.at[place], dst_ref=win_in.at[slot],
            send_sem=win_send.at[place], recv_sem=win_recv.at[slot],
            device_id={"depth": device}, device_id_type=MESH,
        )

    def cut(places):
        across = [one_hot(side, window, offsets[1, place], 0) for place in places]
        strips = dot(field, jnp.concatenate(across, axis=1)).astype(jnp.bfloat16)
        for i, place in enumerate(places):
            strip = strips[:, i * window : (i + 1) * window]
            strip = jnp.concatenate([strip[:side], strip[side:]], axis=1)
            tile = dot(one_hot(side, window, offsets[0, place], 1), strip)
            windows[place, 0] = tile[:, :window]
            windows[place, 1] = tile[:, window:]

    def ship(place, device, slot):
        @pl.when(device != me)
        def _():
            win_copy(place, device, slot).start()

        @pl.when(device == me)
        def _():
            win_in[slot] = windows[place]

    def shipped(place, device, slot):
        @pl.when(device != me)
        def _():
            win_copy(place, device, slot).wait_send()

    loads[0].wait()
    field = obj[...].reshape(2 * side, side)
    for turn in range(0, positions, 2):
        cut([turns[turn][0], turns[turn + 1][0]])
        if turn == 0:
            pl.semaphore_wait(barrier, greetings)
        for near in (turn, turn + 1):
            @pl.when(near < ahead)
            def _():
                ship(*turns[near])

    def ship_rest():
        for turn, target in enumerate(turns):
            @pl.when(turn >= ahead)
            def _():
                ship(*target)

    for load in loads[1:]:
        load.wait()

    def hop(which, peer):
        return pltpu.make_async_remote_copy(
            src_ref=hop_out.at[which], dst_ref=hop_in.at[which],
            send_sem=hop_send.at[which], recv_sem=hop_recv.at[which],
            device_id={"depth": peer}, device_id_type=MESH,
        )

    @pl.when(first)
    def _():
        chosen = ids[mine]
        wave = jnp.zeros(probes.shape[1:], jnp.float32)
        for which in range(probes.shape[0]):
            wave = jnp.where(chosen == which, probes[which], wave)
        waves[0] = wave

    def win_wait(slot):
        @pl.when(low + slot != me)
        def _():
            pltpu.make_async_remote_copy(
                src_ref=windows.at[0], dst_ref=win_in.at[slot],
                send_sem=win_send.at[0], recv_sem=win_recv.at[slot],
                device_id={"depth": low + slot}, device_id_type=MESH,
            ).wait_recv()

    def exit_wave(slot):
        return complex_mul(waves[slot, 0], waves[slot, 1], win_in[slot, 0], win_in[slot, 1])

    def advance(slot):
        real, imag = two_sided(*exit_wave(slot), table, 0)
        waves[slot + 1, 0] = real
        waves[slot + 1, 1] = imag

    def forward(pair, carry):
        win_wait(2 * pair + 1)
        win_wait(2 * pair + 2)
        advance(2 * pair + 1)
        advance(2 * pair + 2)
        return carry

    def grad_copy(slot):
        return pltpu.make_async_remote_copy(
            src_ref=grad_out.at[slot], dst_ref=grads.at[mine],
            send_sem=grad_send.at[slot], recv_sem=grad_recv.at[mine],
            device_id={"depth": low + slot}, device_id_type=MESH,
        )

    def keep_copy(slot):
        return pltpu.make_async_copy(grad_out.at[slot], grads.at[mine], load_sem.at[0])

    def keep_term(slot):
        real, imag = complex_mul(waves[slot, 0], waves[slot, 1], back_buf[0], back_buf[1])
        grad_out[slot, 0] = real
        grad_out[slot, 1] = -imag

    def give(slot):
        @pl.when(low + slot == me)
        def _():
            keep_copy(slot).start()

        @pl.when((low + slot != me) & (low == 0))
        def _():
            grad_copy(slot).start()

    def send_back(slot):
        return two_sided(
            *complex_mul(win_in[slot, 0], win_in[slot, 1], back_buf[0], back_buf[1]), table, 0
        )

    def retreat(slot):
        keep_term(slot)
        real, imag = send_back(slot)
        back_buf[0] = real
        back_buf[1] = imag
        give(slot)

    def backward(pair, carry):
        retreat(slots - 2 - 2 * pair)
        retreat(slots - 3 - 2 * pair)
        return carry

    @pl.when(busy)
    def _():
        @pl.when(low > 0)
        def _():
            hop(0, before).wait_recv()
            waves[0] = hop_in[0]

        win_wait(0)
        advance(0)
        lax.fori_loop(0, slots // 2 - 1, forward, 0)
        win_wait(slots - 1)

        @pl.when(jnp.logical_not(final))
        def _():
            real, imag = two_sided(*exit_wave(slots - 1), table, 0)
            hop_out[0, 0] = real
            hop_out[0, 1] = imag
            hop(0, after).start()

            ship_rest()
            hop(1, after).wait_recv()
            back_buf[0] = hop_in[1, 0]
            back_buf[1] = hop_in[1, 1]

        @pl.when(final)
        def _():
            far_real, far_imag = two_sided(*exit_wave(slots - 1), table, 1)
            excess = far_real * far_real + far_imag * far_imag - measured[...]
            real, imag = two_sided(excess * far_real, -(excess * far_imag), table, 1)
            back_buf[0] = real
            back_buf[1] = imag

        retreat(slots - 1)
        lax.fori_loop(0, slots // 2 - 1, backward, 0)

        @pl.when(low > 0)
        def _():
            real, imag = send_back(0)
            hop_out[1, 0] = real
            hop_out[1, 1] = imag
            hop(1, before).start()

        keep_term(0)
        give(0)

        @pl.when(low > 0)
        def _():
            def late(step, carry):
                slot = slots - 1 - step

                @pl.when(low + slot != me)
                def _():
                    grad_copy(slot).start()

                return carry

            lax.fori_loop(0, slots, late, 0)
            hop(1, before).wait_send()

        @pl.when(jnp.logical_not(final))
        def _():
            hop(0, after).wait_send()

        def sent(slot, carry):
            @pl.when(low + slot != me)
            def _():
                grad_copy(slot).wait_send()

            @pl.when(low + slot == me)
            def _():
                keep_copy(slot).wait()

            return carry

        lax.fori_loop(0, slots, sent, 0)

    for target in turns:
        shipped(*target)

    for place, device, slot in turns:
        @pl.when(device != me)
        def _():
            pltpu.make_async_remote_copy(
                src_ref=grad_out.at[0], dst_ref=grads.at[place],
                send_sem=grad_send.at[0], recv_sem=grad_recv.at[place],
                device_id={"depth": device}, device_id_type=MESH,
            ).wait_recv()


def paint_kernel(offsets, grads, out_hbm, out, total, store_sem):
    positions, window = grads.shape[0], grads.shape[-1]
    side = out.shape[-1]
    total[...] = jnp.zeros_like(total)
    tall, wide = window + 8, 2 * window
    for position in range(positions):
        row, col = offsets[0, position], offsets[1, position]
        row_base = jnp.minimum((row >> 3) << 3, side - tall)
        col_base = jnp.minimum(col // window * window, side - wide)
        rows = pl.ds(pl.multiple_of(row_base, 8), tall)
        cols = pl.ds(pl.multiple_of(col_base, 128), wide)
        for part in range(2):
            tile = grads[position, part]
            tile = jnp.concatenate([tile, jnp.zeros((8, window), jnp.float32)], axis=0)
            tile = pltpu.roll(tile, row - row_base, 0)
            tile = jnp.concatenate([tile, jnp.zeros((tall, window), jnp.float32)], axis=1)
            tile = pltpu.roll(tile, col - col_base, 1)
            total[part, rows, cols] += tile
    pieces = store_sem.shape[0]
    tall = side // pieces
    stores = []
    for piece in range(pieces):
        rows = pl.ds(piece * tall, tall)
        out[:, rows] = total[:, rows].astype(out.dtype)
        stores.append(
            pltpu.make_async_copy(out.at[:, rows], out_hbm.at[0, :, rows], store_sem.at[piece])
        )
        stores[-1].start()
    for store in stores:
        store.wait()


def body(object_slices, probes, measured, scan_offsets, probe_ids, *, count):
    positions, window = measured.shape[0], measured.shape[-1]
    side = object_slices.shape[-1]
    assert count % positions == 0 and positions % 8 == 0
    table = jnp.asarray(tables(window))
    smem = pl.BlockSpec(memory_space=pltpu.SMEM)
    vmem = pl.BlockSpec(memory_space=pltpu.VMEM)
    field = (2, window, window)
    segments = tabulate(plan(count, positions), count)
    longest = max(high - low for _, low, high, _, _ in segments[0])
    stack = pltpu.VMEM((positions,) + field, jnp.float32)
    chain = pltpu.VMEM((longest,) + field, jnp.float32)
    sems = pltpu.SemaphoreType.DMA((positions,))
    chain_sems = pltpu.SemaphoreType.DMA((longest,))
    hbm = pl.BlockSpec(memory_space=pltpu.HBM)
    grads = pl.pallas_call(
        functools.partial(chain_kernel, segments),
        out_shape=pltpu.VMEM((positions,) + field, jnp.float32),
        in_specs=[smem, smem, hbm, hbm, hbm, hbm],
        out_specs=vmem,
        scratch_shapes=[
            pltpu.VMEM(table.shape, jnp.bfloat16),
            pltpu.VMEM(object_slices.shape[1:], jnp.bfloat16),
            pltpu.VMEM(probes.shape, jnp.float32),
            pltpu.VMEM((window, window), jnp.float32),
            stack, chain, chain,
            pltpu.VMEM(field, jnp.float32),
            chain,
            pltpu.VMEM((2,) + field, jnp.float32),
            pltpu.VMEM((2,) + field, jnp.float32),
            sems, chain_sems, chain_sems, sems,
            pltpu.SemaphoreType.DMA((2,)),
            pltpu.SemaphoreType.DMA((2,)),
            pltpu.SemaphoreType.DMA((4,)),
        ],
        compiler_params=pltpu.CompilerParams(
            collective_id=0, has_side_effects=True, vmem_limit_bytes=58 * 1024 * 1024
        ),
    )(scan_offsets.T, probe_ids, object_slices, probes, measured, table)
    return pl.pallas_call(
        paint_kernel,
        out_shape=jax.ShapeDtypeStruct(object_slices.shape, jnp.bfloat16),
        in_specs=[smem, vmem],
        out_specs=hbm,
        scratch_shapes=[
            pltpu.VMEM((2, side, side), jnp.bfloat16),
            pltpu.VMEM((2, side, side), jnp.float32),
            pltpu.SemaphoreType.DMA((4,)),
        ],
        compiler_params=pltpu.CompilerParams(vmem_limit_bytes=32 * 1024 * 1024),
    )(scan_offsets.T, grads)


def solution(mesh):
    return jax.shard_map(
        functools.partial(body, count=mesh.shape["depth"]),
        mesh=mesh,
        in_specs=(
            P(("groups", "depth"), None, None, None),
            P("groups", None, None, None),
            P("groups", None, None),
            P("groups", None),
            P("groups"),
        ),
        out_specs=P(("groups", "depth"), None, None, None),
        check_vma=False,
    )
```

```python
import functools
import math

import jax
import jax.numpy as jnp
import ml_dtypes
import numpy as np
from jax import lax
from jax.experimental import pallas as pl
from jax.experimental.pallas import tpu as pltpu
from jax.sharding import PartitionSpec as P

MESH = pl.DeviceIdType.MESH

PLAN = [[(0, 5)], [(0, 0), (6, 15)], [(0, 7)], [(0, 3), (4, 8)], [(0, 1), (8, 12)], [(0, 6), (4, 10)], [(0, 2), (6, 11)], [(0, 4)]]
RANKS = [[0, 2], [1, 1], [0, 1], [0, 1], [0, 1], [0, 3], [0, 0], [3, 1]]


def split_table(table):
    high = table.astype(ml_dtypes.bfloat16)
    low = (table - high.astype(np.float64)).astype(ml_dtypes.bfloat16)
    return np.stack([high, low])


def right_left(matrix):
    real, imag = matrix.real, matrix.imag
    right = np.block([[real, imag], [-imag, real]])
    left = np.block([[real, -imag], [imag, real]])
    return np.stack([split_table(right), split_table(left)])


def tables(length):
    ordinal = np.arange(length)
    dft = np.exp(-2j * math.pi * (np.outer(ordinal, ordinal) % length) / length) / math.sqrt(length)
    spatial = np.where(ordinal < length // 2, ordinal, ordinal - length)
    chirp = np.exp(-1j * math.pi * (spatial * spatial % (2 * length)) / length)
    prop = (dft.conj() * chirp[None, :]) @ dft
    return np.stack([right_left(prop), right_left(dft)])


def split(values):
    high = values.astype(jnp.bfloat16)
    low = (values - high.astype(jnp.float32)).astype(jnp.bfloat16)
    return high, low


def dot(left, right):
    return jnp.dot(left, right, preferred_element_type=jnp.float32)


def two_sided(real, imag, table_ref, which):
    length = real.shape[0]
    high, low = split(jnp.concatenate([real, imag], axis=1))
    both = dot(jnp.concatenate([high, low], axis=0), table_ref[which, 0, 0])
    mid = both[:length] + both[length:] + dot(high, table_ref[which, 0, 1])
    stacked = jnp.concatenate([mid[:, :length], mid[:, length:]], axis=0)
    high, low = split(stacked)
    both = dot(table_ref[which, 1, 0], jnp.concatenate([high, low], axis=1))
    out = both[:, :length] + both[:, length:] + dot(table_ref[which, 1, 1], high)
    return out[:length], out[length:]


def complex_mul(left_real, left_imag, right_real, right_imag):
    return (
        left_real * right_real - left_imag * right_imag,
        left_real * right_imag + left_imag * right_real,
    )


def one_hot(length, width, start, axis):
    shape = (length, width) if axis == 0 else (width, length)
    place = lax.broadcasted_iota(jnp.int32, shape, axis)
    wanted = lax.broadcasted_iota(jnp.int32, shape, 1 - axis) + start
    return jnp.where(place == wanted, 1.0, 0.0).astype(jnp.bfloat16)


def tuned(count, positions):
    return count == 16 and positions == 8


def plan(count, positions):
    if tuned(count, positions):
        return PLAN
    return [
        [(start, start + position) for start in range(0, count, positions)]
        for position in range(positions)
    ]


def tabulate(segments, count):
    positions = len(segments)
    roles = [(0, 0, 0, -1, -1)] * count
    where = [[None] * positions for _ in range(count)]
    for position, parts in enumerate(segments):
        ends = [start for start, _ in parts[1:]] + [count]
        for i, ((low, device), high) in enumerate(zip(parts, ends)):
            before = parts[i - 1][1] if i > 0 else -1
            after = parts[i + 1][1] if i + 1 < len(parts) else -1
            roles[device] = (position, low, high, before, after)
            for owner in range(low, high):
                where[owner][position] = (device, owner - low)
    orders = [send_order(segments, where, roles, owner) for owner in range(count)]
    peers = [set() for _ in range(count)]
    for owner in range(count):
        for device, _ in where[owner]:
            if device != owner:
                peers[owner].add(device)
                peers[device].add(owner)
    for device, (_, low, high, before, after) in enumerate(roles):
        for other in (before, after):
            if other >= 0:
                peers[device].add(other)
                peers[other].add(device)
    orders, urgent = zip(*orders)
    return roles, where, orders, urgent, [sorted(p) for p in peers]


def send_order(segments, where, roles, owner):
    count = len(where)

    def rank(position):
        device, _ = where[owner][position]
        parts = [i for i, (_, held) in enumerate(segments[position]) if held == device]
        if device // 2 == owner // 2:
            return (0, device != owner, 0, 0)
        return (RANKS[position][parts[0]] if tuned(count, len(segments)) else 0, 1, (device // 2 - owner // 2 - 1) % count, device)

    order = sorted(range(len(segments)), key=rank)
    _, low, high, _, _ = roles[owner]
    if low == 0 and 0 < high < count:
        return order, sum(rank(position)[0] < 2 for position in order)
    return order, len(order)


def chain_kernel(
    segments, offsets, ids, obj_hbm, probes_hbm, measured_hbm, table_hbm,
    grads,
    table, obj, probes, measured, windows, win_in, waves, back_buf, grad_out, hop_out, hop_in,
    win_send, win_recv, grad_send, grad_recv, hop_send, hop_recv, load_sem,
):
    positions, window = measured_hbm.shape[0], measured_hbm.shape[-1]
    side = obj.shape[-1]
    me = lax.axis_index("depth")
    roles, where, orders, urgent, peers = segments
    count = len(roles)

    def look(values):
        found = jnp.int32(values[0])
        for device in range(1, count):
            if values[device] != values[device - 1]:
                found = jnp.where(me >= device, values[device], found)
        return found

    mine, low, high, before, after = (look([role[i] for role in roles]) for i in range(5))
    slots = high - low
    busy = slots > 0
    first = busy & (low == 0)
    final = high == count

    loads = [
        pltpu.make_async_copy(source, target, load_sem.at[i])
        for i, (source, target) in enumerate((
            (obj_hbm.at[0], obj), (table_hbm, table), (probes_hbm, probes),
            (measured_hbm.at[mine], measured),
        ))
    ]
    for load in loads:
        load.start()

    barrier = pltpu.get_barrier_semaphore()
    most = max(len(p) for p in peers)
    for i in range(most):
        peer = look([p[i] if i < len(p) else -1 for p in peers])

        @pl.when(peer >= 0)
        def _():
            pl.semaphore_signal(
                barrier, inc=1, device_id={"depth": peer}, device_id_type=MESH
            )

    greetings = look([len(p) for p in peers])
    ahead = look(urgent)

    turns = []
    for turn in range(positions):
        packed = [
            (orders[d][turn] * count + where[d][orders[d][turn]][0]) * count
            + where[d][orders[d][turn]][1]
            for d in range(count)
        ]
        code = look(packed)
        turns.append((code // (count * count), code // count % count, code % count))

    def win_copy(place, device, slot):
        return pltpu.make_async_remote_copy(
            src_ref=windows.at[place], dst_ref=win_in.at[slot],
            send_sem=win_send.at[place], recv_sem=win_recv.at[slot],
            device_id={"depth": device}, device_id_type=MESH,
        )

    def cut(places):
        across = [one_hot(side, window, offsets[1, place], 0) for place in places]
        strips = dot(field, jnp.concatenate(across, axis=1)).astype(jnp.bfloat16)
        for i, place in enumerate(places):
            strip = strips[:, i * window : (i + 1) * window]
            strip = jnp.concatenate([strip[:side], strip[side:]], axis=1)
            tile = dot(one_hot(side, window, offsets[0, place], 1), strip)
            windows[place, 0] = tile[:, :window]
            windows[place, 1] = tile[:, window:]

    def ship(place, device, slot):
        @pl.when(device != me)
        def _():
            win_copy(place, device, slot).start()

        @pl.when(device == me)
        def _():
            win_in[slot] = windows[place]

    def shipped(place, device, slot):
        @pl.when(device != me)
        def _():
            win_copy(place, device, slot).wait_send()

    loads[0].wait()
    field = obj[...].reshape(2 * side, side)
    for turn in range(0, positions, 2):
        cut([turns[turn][0], turns[turn + 1][0]])
        if turn == 0:
            pl.semaphore_wait(barrier, greetings)
        for near in (turn, turn + 1):
            @pl.when(near < ahead)
            def _():
                ship(*turns[near])

    def ship_rest():
        for turn, target in enumerate(turns):
            @pl.when(turn >= ahead)
            def _():
                ship(*target)

    for load in loads[1:]:
        load.wait()

    def hop(which, peer):
        return pltpu.make_async_remote_copy(
            src_ref=hop_out.at[which], dst_ref=hop_in.at[which],
            send_sem=hop_send.at[which], recv_sem=hop_recv.at[which],
            device_id={"depth": peer}, device_id_type=MESH,
        )

    @pl.when(first)
    def _():
        chosen = ids[mine]
        wave = jnp.zeros(probes.shape[1:], jnp.float32)
        for which in range(probes.shape[0]):
            wave = jnp.where(chosen == which, probes[which], wave)
        waves[0] = wave

    def win_wait(slot):
        @pl.when(low + slot != me)
        def _():
            pltpu.make_async_remote_copy(
                src_ref=windows.at[0], dst_ref=win_in.at[slot],
                send_sem=win_send.at[0], recv_sem=win_recv.at[slot],
                device_id={"depth": low + slot}, device_id_type=MESH,
            ).wait_recv()

    def exit_wave(slot):
        return complex_mul(waves[slot, 0], waves[slot, 1], win_in[slot, 0], win_in[slot, 1])

    def advance(slot):
        real, imag = two_sided(*exit_wave(slot), table, 0)
        waves[slot + 1, 0] = real
        waves[slot + 1, 1] = imag

    def forward(pair, carry):
        win_wait(2 * pair + 1)
        win_wait(2 * pair + 2)
        advance(2 * pair + 1)
        advance(2 * pair + 2)
        return carry

    def grad_copy(slot):
        return pltpu.make_async_remote_copy(
            src_ref=grad_out.at[slot], dst_ref=grads.at[mine],
            send_sem=grad_send.at[slot], recv_sem=grad_recv.at[mine],
            device_id={"depth": low + slot}, device_id_type=MESH,
        )

    def keep_copy(slot):
        return pltpu.make_async_copy(grad_out.at[slot], grads.at[mine], load_sem.at[0])

    def keep_term(slot):
        real, imag = complex_mul(waves[slot, 0], waves[slot, 1], back_buf[0], back_buf[1])
        grad_out[slot, 0] = real
        grad_out[slot, 1] = -imag

    def give(slot):
        @pl.when(low + slot == me)
        def _():
            keep_copy(slot).start()

        @pl.when((low + slot != me) & (low == 0))
        def _():
            grad_copy(slot).start()

    def send_back(slot):
        return two_sided(
            *complex_mul(win_in[slot, 0], win_in[slot, 1], back_buf[0], back_buf[1]), table, 0
        )

    def retreat(slot):
        keep_term(slot)
        give(slot)
        real, imag = send_back(slot)
        back_buf[0] = real
        back_buf[1] = imag

    def backward(pair, carry):
        retreat(slots - 2 - 2 * pair)
        retreat(slots - 3 - 2 * pair)
        return carry

    @pl.when(busy)
    def _():
        @pl.when(low > 0)
        def _():
            hop(0, before).wait_recv()
            waves[0] = hop_in[0]

        win_wait(0)
        advance(0)
        lax.fori_loop(0, slots // 2 - 1, forward, 0)
        win_wait(slots - 1)

        @pl.when(jnp.logical_not(final))
        def _():
            real, imag = two_sided(*exit_wave(slots - 1), table, 0)
            hop_out[0, 0] = real
            hop_out[0, 1] = imag
            hop(0, after).start()

            ship_rest()
            hop(1, after).wait_recv()
            back_buf[0] = hop_in[1, 0]
            back_buf[1] = hop_in[1, 1]

        @pl.when(final)
        def _():
            far_real, far_imag = two_sided(*exit_wave(slots - 1), table, 1)
            excess = far_real * far_real + far_imag * far_imag - measured[...]
            real, imag = two_sided(excess * far_real, -(excess * far_imag), table, 1)
            back_buf[0] = real
            back_buf[1] = imag

        retreat(slots - 1)
        lax.fori_loop(0, slots // 2 - 1, backward, 0)

        @pl.when(low > 0)
        def _():
            real, imag = send_back(0)
            hop_out[1, 0] = real
            hop_out[1, 1] = imag
            hop(1, before).start()

        keep_term(0)
        give(0)

        @pl.when(low > 0)
        def _():
            def late(step, carry):
                slot = slots - 1 - step

                @pl.when(low + slot != me)
                def _():
                    grad_copy(slot).start()

                return carry

            lax.fori_loop(0, slots, late, 0)
            hop(1, before).wait_send()

        @pl.when(jnp.logical_not(final))
        def _():
            hop(0, after).wait_send()

        def sent(slot, carry):
            @pl.when(low + slot != me)
            def _():
                grad_copy(slot).wait_send()

            @pl.when(low + slot == me)
            def _():
                keep_copy(slot).wait()

            return carry

        lax.fori_loop(0, slots, sent, 0)

    for target in turns:
        shipped(*target)

    for place, device, slot in turns:
        @pl.when(device != me)
        def _():
            pltpu.make_async_remote_copy(
                src_ref=grad_out.at[0], dst_ref=grads.at[place],
                send_sem=grad_send.at[0], recv_sem=grad_recv.at[place],
                device_id={"depth": device}, device_id_type=MESH,
            ).wait_recv()


def paint_kernel(offsets, grads, out_hbm, out, total, store_sem):
    positions, window = grads.shape[0], grads.shape[-1]
    side = out.shape[-1]
    total[...] = jnp.zeros_like(total)
    tall, wide = window + 8, 2 * window
    for position in range(positions):
        row, col = offsets[0, position], offsets[1, position]
        row_base = jnp.minimum((row >> 3) << 3, side - tall)
        col_base = jnp.minimum(col // window * window, side - wide)
        rows = pl.ds(pl.multiple_of(row_base, 8), tall)
        cols = pl.ds(pl.multiple_of(col_base, 128), wide)
        for part in range(2):
            tile = grads[position, part]
            tile = jnp.concatenate([tile, jnp.zeros((8, window), jnp.float32)], axis=0)
            tile = pltpu.roll(tile, row - row_base, 0)
            tile = jnp.concatenate([tile, jnp.zeros((tall, window), jnp.float32)], axis=1)
            tile = pltpu.roll(tile, col - col_base, 1)
            total[part, rows, cols] += tile
    pieces = store_sem.shape[0]
    tall = side // pieces
    stores = []
    for piece in range(pieces):
        rows = pl.ds(piece * tall, tall)
        out[:, rows] = total[:, rows].astype(out.dtype)
        stores.append(
            pltpu.make_async_copy(out.at[:, rows], out_hbm.at[0, :, rows], store_sem.at[piece])
        )
        stores[-1].start()
    for store in stores:
        store.wait()


def body(object_slices, probes, measured, scan_offsets, probe_ids, *, count):
    positions, window = measured.shape[0], measured.shape[-1]
    side = object_slices.shape[-1]
    assert count % positions == 0 and positions % 8 == 0
    table = jnp.asarray(tables(window))
    smem = pl.BlockSpec(memory_space=pltpu.SMEM)
    vmem = pl.BlockSpec(memory_space=pltpu.VMEM)
    field = (2, window, window)
    segments = tabulate(plan(count, positions), count)
    longest = max(high - low for _, low, high, _, _ in segments[0])
    stack = pltpu.VMEM((positions,) + field, jnp.float32)
    chain = pltpu.VMEM((longest,) + field, jnp.float32)
    sems = pltpu.SemaphoreType.DMA((positions,))
    chain_sems = pltpu.SemaphoreType.DMA((longest,))
    hbm = pl.BlockSpec(memory_space=pltpu.HBM)
    grads = pl.pallas_call(
        functools.partial(chain_kernel, segments),
        out_shape=pltpu.VMEM((positions,) + field, jnp.float32),
        in_specs=[smem, smem, hbm, hbm, hbm, hbm],
        out_specs=vmem,
        scratch_shapes=[
            pltpu.VMEM(table.shape, jnp.bfloat16),
            pltpu.VMEM(object_slices.shape[1:], jnp.bfloat16),
            pltpu.VMEM(probes.shape, jnp.float32),
            pltpu.VMEM((window, window), jnp.float32),
            stack, chain, chain,
            pltpu.VMEM(field, jnp.float32),
            chain,
            pltpu.VMEM((2,) + field, jnp.float32),
            pltpu.VMEM((2,) + field, jnp.float32),
            sems, chain_sems, chain_sems, sems,
            pltpu.SemaphoreType.DMA((2,)),
            pltpu.SemaphoreType.DMA((2,)),
            pltpu.SemaphoreType.DMA((4,)),
        ],
        compiler_params=pltpu.CompilerParams(
            collective_id=0, has_side_effects=True, vmem_limit_bytes=58 * 1024 * 1024
        ),
    )(scan_offsets.T, probe_ids, object_slices, probes, measured, table)
    return pl.pallas_call(
        paint_kernel,
        out_shape=jax.ShapeDtypeStruct(object_slices.shape, jnp.bfloat16),
        in_specs=[smem, vmem],
        out_specs=hbm,
        scratch_shapes=[
            pltpu.VMEM((2, side, side), jnp.bfloat16),
            pltpu.VMEM((2, side, side), jnp.float32),
            pltpu.SemaphoreType.DMA((4,)),
        ],
        compiler_params=pltpu.CompilerParams(vmem_limit_bytes=32 * 1024 * 1024),
    )(scan_offsets.T, grads)


def solution(mesh):
    return jax.shard_map(
        functools.partial(body, count=mesh.shape["depth"]),
        mesh=mesh,
        in_specs=(
            P(("groups", "depth"), None, None, None),
            P("groups", None, None, None),
            P("groups", None, None),
            P("groups", None),
            P("groups"),
        ),
        out_specs=P(("groups", "depth"), None, None, None),
        check_vma=False,
    )
```
